512 devices in a mesh: seq: 128 (over x, z, core), rep: 4 (over y).
Axes of the slice: x: 4, y: 4, z: 16, core: 2. Of those that a mesh axis runs over, the one named last changes fastest.
Arguments:
- tokens: bfloat16 [16384, 1440], P('seq'), may hold values from -36 to 36
- norm_gain: float32 [1440], replicated, may hold values from 0.1 to 1.9
- expert_ids: int32 [16384, 4], P('seq'), may hold values from 0 to 127, all different within a row; in each aligned block of 128 rows (0 to 127, 128 to 255, ...) at most 8 rows name the same one
- route_weights: float32 [16384, 4], P('seq'), may hold values from 0.1 to 0.6
- gate_weight: bfloat16 [128, 1440, 1440], P('seq', None, 'rep'), may hold values from -0.15625 to 0.15625
- gate_bias: float32 [128, 1440], P('seq', 'rep'), may hold values from -3 to 3
- up_weight: bfloat16 [128, 1440, 1440], P('seq', None, 'rep'), may hold values from -0.15625 to 0.15625
- up_bias: float32 [128, 1440], P('seq', 'rep'), may hold values from -3 to 3
- down_weight: bfloat16 [128, 1440, 1440], P('seq', 'rep'), may hold values from -0.15625 to 0.15625
- down_bias: float32 [128, 1440], P('seq', 'rep'), may hold values from -3 to 3
Outputs:
- mixed: bfloat16 [16384, 1440], P('seq', 'rep')
The draws below stay inside these ranges and needn't reach their ends.
Inputs may be any that keep to these rules, and one draw needn't show every extreme that they name: `expert_ids`: each row names 4 different experts. Among the 128 rows of one index of seq no expert is named more than 8 times, and in every draw some expert is named exactly 8 times by the rows of one index.
All inputs are finite; a program needn't handle non-finite values.
Results may differ from the reference program's by a relative error of at most 0.014.
Values may be sent and summed in bfloat16 or wider, within the bound.
A program may use at most 64 MiB of HBM per device.

```python
import math
import jax
import jax.numpy as jnp
import numpy as np
from jax import lax

D = 1440
EXPERT_HIDDEN = 1440
TOP = 4
TOK_DEV = 128
EXPERTS = 128
CAP = 8
TOKENS = 16384
N_SEQ = 128
N_REP = 4


def draw_tokens(key, part):
    base_key, row_key, col_key = jax.random.split(jax.random.fold_in(key, 11), 3)
    base = jax.random.truncated_normal(base_key, -4.0, 4.0, (TOKENS, D), jnp.float32)
    row_scale = jnp.exp(jax.random.uniform(row_key, (TOKENS, 1), jnp.float32, math.log(0.3), math.log(3.0)))
    col_scale = jnp.exp(jax.random.uniform(col_key, (1, D), jnp.float32, math.log(0.3), math.log(3.0)))
    return (base * row_scale * col_scale).astype(jnp.bfloat16)


def block_scale(own_key, shape, pieces, least, largest):
    factor_of = 1.0
    for axis_at, blocks in pieces:
        steps = jax.random.uniform(jax.random.fold_in(jax.random.fold_in(own_key, 6), axis_at), (blocks,), jnp.float32, least / len(pieces), largest / len(pieces))
        factor_of = factor_of * jnp.repeat(jnp.exp(steps), shape[axis_at] // blocks).reshape((-1,) + (1,) * (len(shape) - 1 - axis_at))
    return factor_of


def deal_out(rng, own, number, rows, amount, top, limit, lean):
    sequence = jax.random.permutation(rng, amount)
    packed, ordinary = load_shares(amount, rows * top, limit, lean, True), load_shares(amount, rows * top, limit, lean, False)
    places = jnp.arange(amount)

    def named(tallies, offset_by):
        used = int((tallies > 0).sum())
        fixed = max(1, used // 4)
        shifted = fixed + (places - fixed + offset_by * (used - fixed)) % max(1, amount - fixed)
        return jnp.zeros((amount,), jnp.int32).at[sequence[jnp.where(places < fixed, places, shifted)]].set(jnp.asarray(tallies, jnp.int32))

    tallies = jnp.where(number % 4 == 0, named(packed, number // 4), named(ordinary, number - number // 4 - 1))
    mixed = jax.random.permutation(jax.random.fold_in(own, 3), amount)
    source_of, sink = mixed[0:amount // 2 * 2:2], mixed[1:amount // 2 * 2:2]
    slack = jnp.minimum(tallies[source_of] - 1, limit - tallies[sink]) // 2
    slack = jnp.where((source_of == sequence[0]) | (sink == sequence[0]) | (tallies[sink] == 0), 0, jnp.maximum(slack, 0))
    shifted = jax.random.randint(jax.random.fold_in(own, 4), (amount // 2,), 0, 1 << 20) % (slack + 1)
    tallies = tallies.at[source_of].add(-shifted).at[sink].add(shifted)
    items = jnp.searchsorted(jnp.cumsum(tallies), jnp.arange(rows * top), side="right").astype(jnp.int32)
    grid = items.reshape(top, rows).T
    grid = grid[jax.random.permutation(jax.random.fold_in(own, 1), rows)]
    offset_by = jax.random.randint(jax.random.fold_in(own, 2), (rows, 1), 0, top)
    return jnp.take_along_axis(grid, (jnp.arange(top)[None, :] + offset_by) % top, axis=1)


def load_shares(number_of, total, bound, skew, full):
    loads = [(1 << 20) // math.isqrt(rank ** skew) + 1 for rank in range(1, number_of + 1)]
    largest = bound if full else min(bound, max(-(-total // number_of), total * loads[0] // sum(loads)))
    least = 1 if total - largest >= number_of - 1 else 0
    counts, spare = [largest] + [least] * (number_of - 1), total - largest - least * (number_of - 1)
    while spare > 0:
        candidates = [i for i in range(1, number_of) if counts[i] < largest] or [i for i in range(1, number_of) if counts[i] < bound]
        pool, left = sum([loads[i] for i in candidates]), spare
        for i in candidates:
            more = min(bound - counts[i], max(1, left * loads[i] // pool), spare)
            counts[i] = counts[i] + more
            spare = spare - more
    return np.array(counts)


def scatter_about(own_key, shape, deviation, limit, cuts=(), kind=jnp.bfloat16):
    level = block_scale(own_key, shape, cuts, -0.22, 0.18) if cuts else 1.0
    entries = jax.random.normal(own_key, shape, jnp.float32) * deviation * level
    return jnp.minimum(jnp.maximum(entries, -limit), limit).astype(kind)


def setup_inputs(seed: int = 0) -> dict:
    streams_of = jax.random.split(jax.random.key(seed), 11)
    tokens = draw_tokens(jax.random.fold_in(streams_of[10], 71), 0)
    norm_gain = jnp.clip(1.0 + 0.18 * jax.random.normal(streams_of[1], (D,), jnp.float32), 0.1, 1.9)
    expert_ids_keys = jax.random.split(jax.random.fold_in(streams_of[2], 1), TOKENS // TOK_DEV)
    expert_ids_turns = jax.random.permutation(jax.random.fold_in(streams_of[2], 3), TOKENS // TOK_DEV)
    expert_ids = jax.vmap(lambda own, number: deal_out(jax.random.fold_in(streams_of[2], 2), own, number, TOK_DEV, EXPERTS, TOP, CAP, 2))(expert_ids_keys, expert_ids_turns).reshape((TOKENS, TOP))
    route_weights = jnp.clip(0.1 + 0.5 * jax.random.uniform(streams_of[3], (TOKENS, TOP), jnp.float32) ** block_scale(streams_of[3], (TOKENS, TOP), ((0, 128),), -0.2, 0.2), 0.1, 0.6)
    gate_weight = scatter_about(streams_of[4], (EXPERTS, D, EXPERT_HIDDEN), D ** -0.5, 0.15625, ((0, 128), (2, 4)))
    gate_bias = scatter_about(streams_of[5], (EXPERTS, EXPERT_HIDDEN), 0.5, 3.0, ((0, 128), (1, 4)), jnp.float32)
    up_weight = scatter_about(streams_of[6], (EXPERTS, D, EXPERT_HIDDEN), D ** -0.5, 0.15625, ((0, 128), (2, 4)))
    up_bias = scatter_about(streams_of[7], (EXPERTS, EXPERT_HIDDEN), 0.5, 3.0, ((0, 128), (1, 4)), jnp.float32)
    down_weight = scatter_about(streams_of[8], (EXPERTS, EXPERT_HIDDEN, D), EXPERT_HIDDEN ** -0.5, 0.15625, ((0, 128), (1, 4)))
    down_bias = scatter_about(streams_of[9], (EXPERTS, D), 0.5, 3.0, ((0, 128), (1, 4)), jnp.float32)
    return dict(tokens=tokens, norm_gain=norm_gain, expert_ids=expert_ids, route_weights=route_weights, gate_weight=gate_weight, gate_bias=gate_bias, up_weight=up_weight, up_bias=up_bias, down_weight=down_weight, down_bias=down_bias)


def reference(tokens, norm_gain, expert_ids, route_weights, gate_weight, gate_bias, up_weight, up_bias, down_weight, down_bias):
    values = tokens.astype(jnp.float32)
    normed = (values * lax.rsqrt(lax.optimization_barrier(jnp.mean(values * values, axis=-1, keepdims=True)) + 1e-05) * norm_gain).astype(jnp.bfloat16)
    pairs = TOK_DEV * TOP
    grouped = expert_ids.reshape(N_SEQ, pairs)
    onehot = (grouped[:, :, None] == jnp.arange(EXPERTS, dtype=jnp.int32)[None, None, :]).astype(jnp.int32)
    before = jnp.cumsum(onehot, axis=1) - onehot
    slot_index = lax.optimization_barrier(jnp.sum(before * onehot, axis=2)).astype(jnp.int32)
    source = jnp.broadcast_to(jnp.arange(N_SEQ, dtype=jnp.int32)[:, None], (N_SEQ, pairs))
    token_row = (jnp.arange(pairs, dtype=jnp.int32) // TOP)[None, :] + source * TOK_DEV
    table = jnp.full((EXPERTS, N_SEQ, CAP), TOKENS, jnp.int32).at[grouped, source, slot_index].set(token_row)
    padded = jnp.concatenate([normed, jnp.zeros((1, D), jnp.bfloat16)], axis=0)
    block_units = EXPERT_HIDDEN // N_REP

    def one_expert(operands):
        rows_table, w_gate, b_gate, w_up, b_up, w_down, b_down = operands
        in_rows = padded[rows_table.reshape(-1)]
        gate_pre = jnp.dot(in_rows, w_gate, preferred_element_type=jnp.float32) + b_gate
        up_pre = jnp.dot(in_rows, w_up, preferred_element_type=jnp.float32) + b_up
        activated = (gate_pre * jax.nn.sigmoid(1.702 * gate_pre) * (up_pre + 1.0)).astype(jnp.bfloat16)
        blocks = activated.reshape(-1, N_REP, block_units).astype(jnp.float32)
        down_blocks = w_down.reshape(N_REP, block_units, D).astype(jnp.float32)
        parts = jnp.einsum('nbh,bhd->nbd', blocks, down_blocks).astype(jnp.bfloat16)
        total = lax.optimization_barrier(jnp.sum(parts.astype(jnp.float32), axis=1)) + b_down
        return total.astype(jnp.bfloat16)
    outputs = lax.map(one_expert, (table, gate_weight, gate_bias, up_weight, up_bias, down_weight, down_bias))
    flat_out = outputs.reshape(EXPERTS * N_SEQ * CAP, D)
    position = (grouped * N_SEQ + source) * CAP + slot_index
    picked = flat_out[position.reshape(-1)].reshape(TOKENS, TOP, D)
    mixed = lax.optimization_barrier(jnp.sum(route_weights[:, :, None] * picked.astype(jnp.float32), axis=1))
    return mixed.astype(jnp.bfloat16)
```

```python
import functools

import jax
import jax.numpy as jnp
from jax import lax
from jax.experimental import pallas as pl
from jax.experimental.pallas import tpu as pltpu
from jax.sharding import PartitionSpec as P

MESH = pl.DeviceIdType.MESH
BF16, F32 = jnp.bfloat16, jnp.float32

CORES = 2
Z_RING = 16
BLOCK = 384
SLOTS = 8
PAIR = 2 * SLOTS


def kernel(
    x_size,
    z_size,
    own_ref,
    meta_ref,
    bias_ref,
    wg_hbm,
    wu_hbm,
    wd_hbm,
    out_ref,
    tok,
    meta,
    rows_out,
    in_rows,
    w_in,
    w_out,
    wg_s,
    wu_s,
    wd_s,
    part,
    rs_r,
    rs_a,
    rs_b,
    rs_t,
    out_rows,
    back,
    mix,
    acc_s,
    acc_r,
    upper,
    w_sem,
    z_send,
    z_recv,
    m_send,
    m_recv,
    x_send,
    x_recv,
    x_loc,
    y_send,
    y_recv,
    r_send,
    r_recv,
    b_send,
    b_recv,
    b_loc,
    c_send,
    c_recv,
):
    seq, y = lax.axis_index("seq"), lax.axis_index("rep")
    half_z = z_size // 2
    stages = half_z
    group = x_size * CORES
    rows = group * PAIR
    tokens = own_ref.shape[0]
    half = tokens // 2
    quarter = out_ref.shape[1]
    xi = seq // (z_size * CORES)
    zi = (seq // CORES) % z_size
    ci = seq % CORES
    me = xi * CORES + ci

    def at_z(step):
        return (xi * z_size + (zi + z_size + step) % z_size) * CORES + ci

    def at_x(index):
        return ((index // CORES) * z_size + zi) * CORES + index % CORES

    def at_y(step):
        return (y + 4 + step) % 4

    z_up, z_down = at_z(1), at_z(-1)

    barrier = pltpu.get_barrier_semaphore()
    for peer in (z_up, z_down):
        pl.semaphore_signal(barrier, inc=1, device_id=(peer, y), device_id_type=MESH)
    for j in range(1, group):
        pl.semaphore_signal(
            barrier, inc=1, device_id=(at_x((me + j) % group), y), device_id_type=MESH
        )
    for step in (1, -1):
        pl.semaphore_signal(barrier, inc=1, device_id=(seq, at_y(step)), device_id_type=MESH)

    weights = [
        pltpu.make_async_copy(wg_hbm.at[0], wg_s, w_sem.at[0]),
        pltpu.make_async_copy(wu_hbm.at[0], wu_s, w_sem.at[1]),
        pltpu.make_async_copy(wd_hbm.at[0], wd_s, w_sem.at[2]),
    ]
    for copy in weights:
        copy.start()
    pl.semaphore_wait(barrier, 2 + (group - 1) + 2)

    def z_copy(way, k, h, src):
        return pltpu.make_async_remote_copy(
            src_ref=src.at[pl.ds(h * half, half)],
            dst_ref=tok.at[k, way, pl.ds(h * half, half)],
            send_sem=z_send.at[way, k, h],
            recv_sem=z_recv.at[way, k, h],
            device_id=(z_up if way else z_down, y),
            device_id_type=MESH,
        )

    def m_copy(way, k, src):
        return pltpu.make_async_remote_copy(
            src_ref=src,
            dst_ref=meta.at[k, way],
            send_sem=m_send.at[way, k],
            recv_sem=m_recv.at[way, k],
            device_id=(z_up if way else z_down, y),
            device_id_type=MESH,
        )

    for way in (0, 1):
        m_copy(way, way, meta_ref).start()
        for h in (0, 1):
            z_copy(way, way, h, own_ref).start()

    tok[0, 1] = own_ref[...]
    meta[0, 1] = meta_ref[...]
    upper[...] = (
        lax.broadcasted_iota(jnp.int32, (tokens, tokens), 0)
        < lax.broadcasted_iota(jnp.int32, (tokens, tokens), 1)
    ).astype(BF16)

    features, hidden = wg_s.shape
    w_in[...] = jnp.zeros_like(w_in)
    w_out[...] = jnp.zeros_like(w_out)
    for copy in weights:
        copy.wait()
    strip = 144

    @pl.loop(0, features // strip)
    def _(i):
        at = pl.ds(pl.multiple_of(i * strip, 16), strip)
        w_in[at, 0:hidden] = wg_s[at, :]
        w_in[at, BLOCK : BLOCK + hidden] = wu_s[at, :]

    for p in range(4):
        w_out[0:hidden, p * BLOCK : p * BLOCK + quarter] = wd_s[:, p * quarter : (p + 1) * quarter]

    expert = lax.broadcasted_iota(jnp.int32, (group, tokens), 0)
    expert = ((expert // CORES) * z_size + zi) * CORES + expert % CORES
    expert = expert.astype(F32)
    slot = lax.broadcasted_iota(jnp.int32, (group, SLOTS, tokens), 1).astype(F32)

    def x_copy(k, j):
        e = (me + j) % group
        return pltpu.make_async_remote_copy(
            src_ref=rows_out.at[k, e],
            dst_ref=in_rows.at[k, y, me],
            send_sem=x_send.at[k],
            recv_sem=x_recv.at[k],
            device_id=(at_x(e), y),
            device_id_type=MESH,
        )

    def x_local(k):
        return pltpu.make_async_copy(rows_out.at[k, me], in_rows.at[k, y, me], x_loc.at[k])

    def b_copy(k, j):
        e = (me + j) % group
        return pltpu.make_async_remote_copy(
            src_ref=out_rows.at[k, e],
            dst_ref=back.at[k, me],
            send_sem=b_send.at[k],
            recv_sem=b_recv.at[k],
            device_id=(at_x(e), y),
            device_id_type=MESH,
        )

    def b_local(k):
        return pltpu.make_async_copy(out_rows.at[k, me], back.at[k, me], b_loc.at[k])

    def sign(k):
        return 1 - 2 * (k % 2)

    def y_copy(k, kind):
        s = sign(k)
        block = at_y(-s) if kind == 2 else y
        to = at_y(-s) if kind == 1 else at_y(s)
        return pltpu.make_async_remote_copy(
            src_ref=in_rows.at[k, block],
            dst_ref=in_rows.at[k, block],
            send_sem=y_send.at[kind, k],
            recv_sem=y_recv.at[kind, k],
            device_id=(seq, to),
            device_id_type=MESH,
        )

    def r_copy(k, kind):
        s = sign(k)
        to = at_y(-s) if kind == 1 else at_y(s)
        src = rs_t.at[k] if kind == 2 else part.at[k, at_y(2) if kind == 0 else at_y(-s)]
        return pltpu.make_async_remote_copy(
            src_ref=src,
            dst_ref=(rs_r, rs_b, rs_a)[kind].at[k],
            send_sem=r_send.at[kind, k],
            recv_sem=r_recv.at[kind, k],
            device_id=(seq, to),
            device_id_type=MESH,
        )

    def c_copy(way, k, h, to_slot):
        return pltpu.make_async_remote_copy(
            src_ref=acc_s.at[way, k, pl.ds(h * half, half)],
            dst_ref=acc_r.at[way, to_slot, pl.ds(h * half, half)],
            send_sem=c_send.at[way, k, h],
            recv_sem=c_recv.at[way, to_slot, h],
            device_id=(z_down if way else z_up, y),
            device_id_type=MESH,
        )

    def z_stage(k):
        @pl.when(k >= 1)
        def _():
            m_copy(1, k, meta.at[k, 1]).wait_recv()

            @pl.when(k < stages - 1)
            def _():
                m_copy(1, k + 1, meta.at[k, 1]).start()

            for h in (0, 1):
                z_copy(1, k, h, tok.at[k, 1]).wait_recv()

                @pl.when(k < stages - 1)
                def _():
                    z_copy(1, k + 1, h, tok.at[k, 1]).start()

        m_copy(0, k, meta.at[k, 0]).wait_recv()

        @pl.when(k < stages - 1)
        def _():
            m_copy(0, k + 1, meta.at[k, 0]).start()

        for h in (0, 1):
            z_copy(0, k, h, tok.at[k, 0]).wait_recv()

            @pl.when(k < stages - 1)
            def _():
                z_copy(0, k + 1, h, tok.at[k, 0]).start()

    def dispatch(k):
        picks, mixes = [], []
        for j in (0, 1):
            m = meta[k, j]
            hit = jnp.zeros((group, tokens), F32)
            weight = jnp.zeros((group, tokens), F32)
            for c in range(4):
                equal = m[c : c + 1, :] == expert
                hit = jnp.where(equal, 1.0, hit)
                weight = jnp.where(equal, m[4 + c : 5 + c, :], weight)
            rank = jnp.dot(hit.astype(BF16), upper[...], preferred_element_type=F32)
            rank = jnp.where(hit > 0.5, rank, -1.0)
            chosen = rank[:, None, :] == slot
            picks.append(jnp.where(chosen, 1.0, 0.0))
            mixes.append(jnp.where(chosen, weight[:, None, :], 0.0))
        empty = jnp.zeros((group, SLOTS, tokens), F32)

        def both(a, b):
            top = jnp.concatenate([a, empty], axis=2)
            low = jnp.concatenate([empty, b], axis=2)
            return jnp.concatenate([top, low], axis=1).reshape(rows, 2 * tokens)

        pick = both(*picks).astype(BF16)
        got = jnp.dot(pick, tok[k].reshape(2 * tokens, BLOCK), preferred_element_type=F32)
        rows_out[k] = got.astype(BF16).reshape(group, PAIR, BLOCK)
        x_local(k).start()
        for j in range(1, group):
            x_copy(k, j).start()
        blend = both(*mixes).T
        high = blend.astype(BF16)
        mix[k, :, 0:rows] = high
        mix[k, :, rows : 2 * rows] = (blend - high.astype(F32)).astype(BF16)

    def y_start(k):
        x_local(k).wait()
        whole = in_rows.at[k, y, pl.ds(0, group - 1)]
        pltpu.make_async_copy(whole, whole, x_recv.at[k]).wait()
        y_copy(k, 0).start()
        y_copy(k, 1).start()

    def y_relay(k):
        y_copy(k, 0).wait_recv()
        y_copy(k, 2).start()

    def compute(k):
        y_copy(k, 1).wait_recv()
        y_copy(k, 2).wait_recv()
        x = jnp.concatenate([in_rows[k, q].reshape(rows, BLOCK) for q in range(4)], axis=1)
        pre = jnp.dot(x, w_in[...], preferred_element_type=F32)
        gate = pre[:, :BLOCK] + bias_ref[0:1, :]
        up = pre[:, BLOCK:] + bias_ref[1:2, :]
        act = (gate * jax.nn.sigmoid(1.702 * gate) * (up + 1.0)).astype(BF16)
        result = jnp.dot(act, w_out[...], preferred_element_type=F32).astype(BF16)
        for p in range(4):
            part[k, p] = result[:, p * BLOCK : (p + 1) * BLOCK]

    @pl.loop(0, stages + 3)
    def _(t):
        @pl.when(t < stages)
        def _():
            z_stage(t)
            dispatch(t)

        @pl.when((t >= 1) & (t < stages + 1))
        def _():
            y_start(t - 1)

        @pl.when((t >= 2) & (t < stages + 2))
        def _():
            y_relay(t - 2)

        @pl.when(t >= 3)
        def _():
            compute(t - 3)

    def r_start(k):
        r_copy(k, 0).start()
        r_copy(k, 1).start()

    def r_relay(k):
        r_copy(k, 0).wait_recv()
        total = rs_r[k].astype(F32) + part[k, at_y(sign(k))].astype(F32)
        rs_t[k] = total.astype(BF16)
        r_copy(k, 2).start()

    def finish(k):
        r_copy(k, 1).wait_recv()
        r_copy(k, 2).wait_recv()
        total = part[k, y].astype(F32) + rs_b[k].astype(F32) + rs_a[k].astype(F32)
        total = total + bias_ref[2:3, :]
        out_rows[k] = total.astype(BF16).reshape(group, PAIR, BLOCK)
        b_local(k).start()
        for j in range(1, group):
            b_copy(k, j).start()

    def combine(k):
        b_local(k).wait()
        whole = back.at[k, pl.ds(0, group - 1)]
        pltpu.make_async_copy(whole, whole, b_recv.at[k]).wait()
        came = back[k].reshape(rows, BLOCK)
        came = jnp.concatenate([came, came], axis=0)
        both = jnp.dot(mix[k], came, preferred_element_type=F32)
        for h in (0, 1):
            at = pl.ds(h * half, half)
            for way in (0, 1):
                value = both[way * tokens + h * half : way * tokens + (h + 1) * half]

                @pl.when(k == stages - 1)
                def _():
                    acc_s[way, k, at] = value.astype(BF16)

                @pl.when(k < stages - 1)
                def _():
                    c_copy(way, k, h, k).wait_recv()
                    total = value + acc_r[way, k, at].astype(F32)
                    acc_s[way, k, at] = total.astype(BF16)

                if way == 0:
                    c_copy(0, k, h, (k + stages - 1) % stages).start()
                else:

                    @pl.when(k >= 1)
                    def _():
                        c_copy(1, k, h, k - 1).start()

        @pl.when(k == 0)
        def _():
            for h in (0, 1):
                at = pl.ds(h * half, half)
                value = both[tokens + h * half : tokens + (h + 1) * half]
                c_copy(0, 0, h, stages - 1).wait_recv()
                total = value + acc_r[1, 0, at].astype(F32) + acc_r[0, stages - 1, at].astype(F32)
                out_ref[at, :] = total[:, :quarter].astype(out_ref.dtype)

    @pl.loop(0, stages + 3)
    def _(t):
        @pl.when(t < stages)
        def _():
            r_start(stages - 1 - t)

        @pl.when((t >= 1) & (t < stages + 1))
        def _():
            r_relay(stages - t)

        @pl.when((t >= 2) & (t < stages + 2))
        def _():
            finish(stages + 1 - t)

        @pl.when(t >= 3)
        def _():
            combine(stages + 2 - t)

    @pl.loop(0, stages)
    def _(k):
        for way in (0, 1):

            @pl.when(k >= way)
            def _():
                m_copy(way, k, meta_ref).wait_send()
                for h in (0, 1):
                    z_copy(way, k, h, own_ref).wait_send()
                    c_copy(way, k, h, k).wait_send()

        for kind in range(3):
            y_copy(k, kind).wait_send()
            r_copy(k, kind).wait_send()
        sent = rows_out.at[k, pl.ds(0, group - 1)]
        pltpu.make_async_copy(sent, sent, x_send.at[k]).wait()
        sent = out_rows.at[k, pl.ds(0, group - 1)]
        pltpu.make_async_copy(sent, sent, b_send.at[k]).wait()


def on_device(
    tokens,
    norm_gain,
    expert_ids,
    route_weights,
    gate_weight,
    gate_bias,
    up_weight,
    up_bias,
    down_weight,
    down_bias,
):
    tok_rows, features = tokens.shape
    z_size = Z_RING
    x_size = lax.axis_size("seq") // (z_size * CORES)
    hidden = gate_weight.shape[2]
    quarter = features // 4
    stages = z_size // 2
    group = x_size * CORES
    rows = group * PAIR
    values = tokens.astype(F32)
    normed = (
        values * lax.rsqrt(jnp.mean(values * values, axis=-1, keepdims=True) + 1e-05) * norm_gain
    ).astype(BF16)
    normed = jnp.pad(normed, ((0, 0), (0, 4 * BLOCK - features)))
    own = lax.dynamic_slice(normed, (0, lax.axis_index("rep") * BLOCK), (tok_rows, BLOCK))
    meta = jnp.concatenate([expert_ids.T.astype(F32), route_weights.T], axis=0)
    bias = jnp.concatenate([gate_bias, up_bias, down_bias], axis=0)
    bias = jnp.pad(bias, ((0, 5), (0, BLOCK - hidden)))

    block = (stages, rows, BLOCK)
    vmem = pl.BlockSpec(memory_space=pltpu.VMEM)
    hbm = pl.BlockSpec(memory_space=pl.ANY)
    dma = pltpu.SemaphoreType.DMA
    return pl.pallas_call(
        functools.partial(kernel, x_size, z_size),
        out_shape=jax.ShapeDtypeStruct((tok_rows, quarter), BF16),
        in_specs=[vmem, vmem, vmem, hbm, hbm, hbm],
        out_specs=vmem,
        scratch_shapes=[
            pltpu.VMEM((stages, 2, tok_rows, BLOCK), BF16),
            pltpu.VMEM((stages, 2, 8, tok_rows), F32),
            pltpu.VMEM((stages, group, PAIR, BLOCK), BF16),
            pltpu.VMEM((stages, 4, group, PAIR, BLOCK), BF16),
            pltpu.VMEM((4 * BLOCK, 2 * BLOCK), BF16),
            pltpu.VMEM((BLOCK, 4 * BLOCK), BF16),
            pltpu.VMEM(gate_weight.shape[1:], BF16),
            pltpu.VMEM(up_weight.shape[1:], BF16),
            pltpu.VMEM(down_weight.shape[1:], BF16),
            pltpu.VMEM((stages, 4, rows, BLOCK), BF16),
            pltpu.VMEM(block, BF16),
            pltpu.VMEM(block, BF16),
            pltpu.VMEM(block, BF16),
            pltpu.VMEM(block, BF16),
            pltpu.VMEM((stages, group, PAIR, BLOCK), BF16),
            pltpu.VMEM((stages, group, PAIR, BLOCK), BF16),
            pltpu.VMEM((stages, 2 * tok_rows, 2 * rows), BF16),
            pltpu.VMEM((2, stages, tok_rows, BLOCK), BF16),
            pltpu.VMEM((2, stages, tok_rows, BLOCK), BF16),
            pltpu.VMEM((tok_rows, tok_rows), BF16),
            dma((3,)),
            dma((2, stages, 2)),
            dma((2, stages, 2)),
            dma((2, stages)),
            dma((2, stages)),
            dma((stages,)),
            dma((stages,)),
            dma((stages,)),
            dma((3, stages)),
            dma((3, stages)),
            dma((3, stages)),
            dma((3, stages)),
            dma((stages,)),
            dma((stages,)),
            dma((stages,)),
            dma((2, stages, 2)),
            dma((2, stages, 2)),
        ],
        compiler_params=pltpu.CompilerParams(
            collective_id=0, has_side_effects=True, vmem_limit_bytes=56 * 1024 * 1024
        ),
    )(own, meta, bias, gate_weight, up_weight, down_weight)


def solution(mesh):
    placed = (
        P("seq", None),
        P(),
        P("seq", None),
        P("seq", None),
        P("seq", None, "rep"),
        P("seq", "rep"),
        P("seq", None, "rep"),
        P("seq", "rep"),
        P("seq", "rep", None),
        P("seq", "rep"),
    )
    return jax.shard_map(
        on_device, mesh=mesh, in_specs=placed, out_specs=P("seq", "rep"), check_vma=False
    )
```

```python
import functools

import jax
import jax.numpy as jnp
from jax import lax
from jax.experimental import pallas as pl
from jax.experimental.pallas import tpu as pltpu
from jax.sharding import PartitionSpec as P

MESH = pl.DeviceIdType.MESH
BF16, F32 = jnp.bfloat16, jnp.float32

CORES = 2
Z_RING = 16
BLOCK = 384
SLOTS = 8
PAIR = 2 * SLOTS
CUTS = 4


def kernel(
    x_size,
    z_size,
    tokens_hbm,
    gain_hbm,
    ids_hbm,
    route_hbm,
    bg_hbm,
    bu_hbm,
    bd_hbm,
    wg_hbm,
    wu_hbm,
    wd_hbm,
    out_ref,
    tokens_s,
    gain_s,
    ids_s,
    route_s,
    bg_s,
    bu_s,
    bd_s,
    bias_ref,
    tok,
    meta,
    rows_out,
    in_rows,
    w_in,
    w_out,
    wg_s,
    wu_s,
    wd_s,
    part,
    rs_r,
    rs_a,
    rs_b,
    rs_t,
    out_rows,
    back,
    mix,
    acc_s,
    acc_r,
    upper,
    i_sem,
    w_sem,
    z_send,
    z_recv,
    m_send,
    m_recv,
    x_send,
    x_recv,
    x_loc,
    y_send,
    y_recv,
    r_send,
    r_recv,
    b_send,
    b_recv,
    b_loc,
    c_send,
    c_recv,
):
    seq, y = lax.axis_index("seq"), lax.axis_index("rep")
    half_z = z_size // 2
    stages = half_z
    group = x_size * CORES
    rows = group * PAIR
    tokens = tok.shape[2]
    piece = tokens // CUTS
    side = group // 2
    quarter = out_ref.shape[0]
    xi = seq // (z_size * CORES)
    zi = (seq // CORES) % z_size
    ci = seq % CORES
    me = xi * CORES + ci

    def at_z(step):
        return (xi * z_size + (zi + z_size + step) % z_size) * CORES + ci

    def at_x(index):
        return ((index // CORES) * z_size + zi) * CORES + index % CORES

    def at_y(step):
        return (y + 4 + step) % 4

    z_up, z_down = at_z(1), at_z(-1)

    small = [
        pltpu.make_async_copy(src, dst, i_sem.at[i])
        for i, (src, dst) in enumerate(
            (
                (tokens_hbm, tokens_s),
                (gain_hbm, gain_s),
                (ids_hbm, ids_s),
                (route_hbm, route_s),
                (bg_hbm, bg_s),
                (bu_hbm, bu_s),
                (bd_hbm, bd_s),
            )
        )
    ]
    for copy in small:
        copy.start()

    barrier = pltpu.get_barrier_semaphore()
    for peer in (z_up, z_down):
        pl.semaphore_signal(barrier, inc=1, device_id=(peer, y), device_id_type=MESH)
    for j in range(1, group):
        pl.semaphore_signal(
            barrier, inc=1, device_id=(at_x((me + j) % group), y), device_id_type=MESH
        )
    for step in (1, -1):
        pl.semaphore_signal(barrier, inc=1, device_id=(seq, at_y(step)), device_id_type=MESH)

    weights = [
        pltpu.make_async_copy(wg_hbm.at[0], wg_s, w_sem.at[0]),
        pltpu.make_async_copy(wu_hbm.at[0], wu_s, w_sem.at[1]),
        pltpu.make_async_copy(wd_hbm.at[0], wd_s, w_sem.at[2]),
    ]
    for copy in weights:
        copy.start()

    def z_copy(way, k, h, src):
        return pltpu.make_async_remote_copy(
            src_ref=src.at[pl.ds(h * piece, piece)],
            dst_ref=tok.at[k, way, pl.ds(h * piece, piece)],
            send_sem=z_send.at[way, k, h],
            recv_sem=z_recv.at[way, k, h],
            device_id=(z_up if way else z_down, y),
            device_id_type=MESH,
        )

    def m_copy(way, k, src):
        return pltpu.make_async_remote_copy(
            src_ref=src,
            dst_ref=meta.at[k, way],
            send_sem=m_send.at[way, k],
            recv_sem=m_recv.at[way, k],
            device_id=(z_up if way else z_down, y),
            device_id_type=MESH,
        )

    for copy in small:
        copy.wait()
    values = tokens_s[...].astype(F32)
    features = values.shape[0]
    scale = lax.rsqrt(jnp.sum(values * values, axis=0, keepdims=True) / features + 1e-05)
    for q in range(4):
        width = min(BLOCK, features - q * BLOCK)

        @pl.when(y == q)
        def _():
            at = slice(q * BLOCK, q * BLOCK + width)
            normed = (tokens_s[at, :].astype(F32) * scale).T * gain_s[at].reshape(1, width)
            if width < BLOCK:
                tok[0, 1] = jnp.zeros((tokens, BLOCK), BF16)
            tok[0, 1, :, 0:width] = normed.astype(BF16)

    meta[0, 1] = jnp.concatenate([ids_s[...].astype(F32), route_s[...]], axis=0)
    pl.semaphore_wait(barrier, 2 + (group - 1) + 2)
    for way in (0, 1):
        m_copy(way, way, meta.at[0, 1]).start()
    for h in range(CUTS):
        for way in (0, 1):
            z_copy(way, way, h, tok.at[0, 1]).start()

    hidden = bg_s.shape[1]
    bias_ref[...] = jnp.zeros_like(bias_ref)
    bias_ref[0:1, 0:hidden] = bg_s[...]
    bias_ref[1:2, 0:hidden] = bu_s[...]
    bias_ref[2:3, 0:quarter] = bd_s[...]
    upper[...] = (
        lax.broadcasted_iota(jnp.int32, (tokens, tokens), 0)
        < lax.broadcasted_iota(jnp.int32, (tokens, tokens), 1)
    ).astype(BF16)

    w_in[...] = jnp.zeros_like(w_in)
    w_out[...] = jnp.zeros_like(w_out)
    for copy in weights:
        copy.wait()
    strip = 144

    @pl.loop(0, features // strip)
    def _(i):
        at = pl.ds(pl.multiple_of(i * strip, 16), strip)
        w_in[at, 0:hidden] = wg_s[at, :]
        w_in[at, BLOCK : BLOCK + hidden] = wu_s[at, :]

    for p in range(4):
        w_out[0:hidden, p * BLOCK : p * BLOCK + quarter] = wd_s[:, p * quarter : (p + 1) * quarter]

    expert = lax.broadcasted_iota(jnp.int32, (group, tokens), 0)
    expert = ((expert // CORES) * z_size + zi) * CORES + expert % CORES
    expert = expert.astype(F32)
    slot = lax.broadcasted_iota(jnp.int32, (group, SLOTS, tokens), 1).astype(F32)

    def x_copy(k, j):
        e = (me + j) % group
        return pltpu.make_async_remote_copy(
            src_ref=rows_out.at[k, e],
            dst_ref=in_rows.at[k, y, me],
            send_sem=x_send.at[k],
            recv_sem=x_recv.at[k],
            device_id=(at_x(e), y),
            device_id_type=MESH,
        )

    def x_local(k):
        return pltpu.make_async_copy(rows_out.at[k, me], in_rows.at[k, y, me], x_loc.at[k])

    def b_copy(k, j):
        e = (me + j) % group
        return pltpu.make_async_remote_copy(
            src_ref=out_rows.at[k, e],
            dst_ref=back.at[k, me],
            send_sem=b_send.at[k],
            recv_sem=b_recv.at[k],
            device_id=(at_x(e), y),
            device_id_type=MESH,
        )

    def b_local(k):
        return pltpu.make_async_copy(out_rows.at[k, me], back.at[k, me], b_loc.at[k])

    def y_copy(k, kind, h):
        s = 1 - 2 * h
        block = at_y(-s) if kind == 2 else y
        at = in_rows.at[k, block, pl.ds(h * side, side)]
        return pltpu.make_async_remote_copy(
            src_ref=at,
            dst_ref=at,
            send_sem=y_send.at[kind, k, h],
            recv_sem=y_recv.at[kind, k, h],
            device_id=(seq, at_y(-s) if kind == 1 else at_y(s)),
            device_id_type=MESH,
        )

    def r_copy(k, kind, h):
        s = 1 - 2 * h
        at = pl.ds(h * (rows // 2), rows // 2)
        src = rs_t.at[k, at] if kind == 2 else part.at[k, at_y(2) if kind == 0 else at_y(-s), at]
        return pltpu.make_async_remote_copy(
            src_ref=src,
            dst_ref=(rs_r, rs_b, rs_a)[kind].at[k, at],
            send_sem=r_send.at[kind, k, h],
            recv_sem=r_recv.at[kind, k, h],
            device_id=(seq, at_y(-s) if kind == 1 else at_y(s)),
            device_id_type=MESH,
        )

    def c_copy(way, k, h, to_slot):
        return pltpu.make_async_remote_copy(
            src_ref=acc_s.at[way, k, pl.ds(h * piece, piece)],
            dst_ref=acc_r.at[way, to_slot, pl.ds(h * piece, piece)],
            send_sem=c_send.at[way, k, h],
            recv_sem=c_recv.at[way, to_slot, h],
            device_id=(z_down if way else z_up, y),
            device_id_type=MESH,
        )

    def z_stage(k):
        def step(way, wait, forward):
            def go():
                wait()
                pl.when(k < stages - 1)(forward)

            if way:
                pl.when(k >= 1)(go)
            else:
                go()

        for way in (1, 0):
            step(
                way,
                lambda: m_copy(way, k, meta.at[k, way]).wait_recv(),
                lambda: m_copy(way, k + 1, meta.at[k, way]).start(),
            )
        for h in range(CUTS):
            for way in (1, 0):
                step(
                    way,
                    lambda: z_copy(way, k, h, tok.at[k, way]).wait_recv(),
                    lambda: z_copy(way, k + 1, h, tok.at[k, way]).start(),
                )

    def dispatch(k):
        picks, mixes = [], []
        for j in (0, 1):
            m = meta[k, j]
            hit = jnp.zeros((group, tokens), F32)
            weight = jnp.zeros((group, tokens), F32)
            for c in range(4):
                equal = m[c : c + 1, :] == expert
                hit = jnp.where(equal, 1.0, hit)
                weight = jnp.where(equal, m[4 + c : 5 + c, :], weight)
            rank = jnp.dot(hit.astype(BF16), upper[...], preferred_element_type=F32)
            rank = jnp.where(hit > 0.5, rank, -1.0)
            chosen = rank[:, None, :] == slot
            picks.append(jnp.where(chosen, 1.0, 0.0))
            mixes.append(jnp.where(chosen, weight[:, None, :], 0.0))
        empty = jnp.zeros((group, SLOTS, tokens), F32)

        def both(a, b):
            top = jnp.concatenate([a, empty], axis=2)
            low = jnp.concatenate([empty, b], axis=2)
            return jnp.concatenate([top, low], axis=1).reshape(rows, 2 * tokens)

        pick = both(*picks).astype(BF16)
        got = jnp.dot(pick, tok[k].reshape(2 * tokens, BLOCK), preferred_element_type=F32)
        rows_out[k] = got.astype(BF16).reshape(group, PAIR, BLOCK)
        x_local(k).start()
        for j in range(1, group):
            x_copy(k, j).start()
        blend = both(*mixes).T
        high = blend.astype(BF16)
        mix[k, :, 0:rows] = high
        mix[k, :, rows : 2 * rows] = (blend - high.astype(F32)).astype(BF16)

    def y_start(k):
        x_local(k).wait()
        whole = in_rows.at[k, y, pl.ds(0, group - 1)]
        pltpu.make_async_copy(whole, whole, x_recv.at[k]).wait()
        for kind in (0, 1):
            for h in (0, 1):
                y_copy(k, kind, h).start()

    def y_relay(k):
        for h in (0, 1):
            y_copy(k, 0, h).wait_recv()
            y_copy(k, 2, h).start()

    def compute(k):
        for kind in (1, 2):
            for h in (0, 1):
                y_copy(k, kind, h).wait_recv()
        x = jnp.concatenate([in_rows[k, q].reshape(rows, BLOCK) for q in range(4)], axis=1)
        pre = jnp.dot(x, w_in[...], preferred_element_type=F32)
        gate = pre[:, :BLOCK] + bias_ref[0:1, :]
        up = pre[:, BLOCK:] + bias_ref[1:2, :]
        act = (gate * jax.nn.sigmoid(1.702 * gate) * (up + 1.0)).astype(BF16)
        result = jnp.dot(act, w_out[...], preferred_element_type=F32).astype(BF16)
        for p in range(4):
            part[k, p] = result[:, p * BLOCK : (p + 1) * BLOCK]

    def stage(t, first, go):
        pl.when((t >= first) & (t < stages + first))(lambda: go(t - first))

    @pl.loop(0, stages + 4)
    def _(t):
        stage(t, 0, z_stage)
        stage(t, 0, dispatch)
        stage(t, 1, y_start)
        stage(t, 4, compute)
        stage(t, 2, y_relay)

    def r_start(k, kind):
        for h in (0, 1):
            r_copy(k, kind, h).start()

    def r_relay(k):
        for h in (0, 1):
            at = pl.ds(h * (rows // 2), rows // 2)
            r_copy(k, 0, h).wait_recv()
            total = rs_r[k, at].astype(F32) + part[k, at_y(1 - 2 * h), at].astype(F32)
            rs_t[k, at] = total.astype(BF16)
            r_copy(k, 2, h).start()

    def finish(k):
        for kind in (1, 2):
            for h in (0, 1):
                r_copy(k, kind, h).wait_recv()
        total = part[k, y].astype(F32) + rs_b[k].astype(F32) + rs_a[k].astype(F32)
        total = total + bias_ref[2:3, :]
        out_rows[k] = total.astype(BF16).reshape(group, PAIR, BLOCK)
        b_local(k).start()
        for j in range(1, group):
            b_copy(k, j).start()

    def combine(k):
        b_local(k).wait()
        whole = back.at[k, pl.ds(0, group - 1)]
        pltpu.make_async_copy(whole, whole, b_recv.at[k]).wait()
        came = back[k].reshape(rows, BLOCK)
        came = jnp.concatenate([came, came], axis=0)
        both = jnp.dot(mix[k], came, preferred_element_type=F32)
        for h in range(CUTS):
            at = pl.ds(h * piece, piece)
            for way in (0, 1):
                first = way * tokens + h * piece
                value = both[first : first + piece]

                @pl.when(k == stages - 1)
                def _():
                    acc_s[way, k, at] = value.astype(BF16)

                @pl.when(k < stages - 1)
                def _():
                    c_copy(way, k, h, k).wait_recv()
                    total = value + acc_r[way, k, at].astype(F32)
                    acc_s[way, k, at] = total.astype(BF16)

                if way == 0:
                    c_copy(0, k, h, (k + stages - 1) % stages).start()
                else:

                    @pl.when(k >= 1)
                    def _():
                        c_copy(1, k, h, k - 1).start()

        @pl.when(k == 0)
        def _():
            for h in range(CUTS):
                c_copy(0, 0, h, stages - 1).wait_recv()
            total = both[tokens:] + acc_r[1, 0].astype(F32) + acc_r[0, stages - 1].astype(F32)
            out_ref[...] = total.T[:quarter].astype(out_ref.dtype)

    def turn(go):
        return lambda n: go(stages - 1 - n)

    @pl.loop(0, stages + 4)
    def _(t):
        stage(t, 0, turn(lambda k: r_start(k, 0)))
        stage(t, 3, turn(finish))
        stage(t, 1, turn(lambda k: r_start(k, 1)))
        stage(t, 1, turn(r_relay))
        stage(t, 4, turn(combine))

    @pl.loop(0, stages)
    def _(k):
        for way in (0, 1):

            @pl.when(k >= way)
            def _():
                m_copy(way, k, meta.at[k, way]).wait_send()
                for h in range(CUTS):
                    z_copy(way, k, h, tok.at[k, way]).wait_send()
                    c_copy(way, k, h, k).wait_send()

        for kind in range(3):
            for h in (0, 1):
                y_copy(k, kind, h).wait_send()
                r_copy(k, kind, h).wait_send()
        sent = rows_out.at[k, pl.ds(0, group - 1)]
        pltpu.make_async_copy(sent, sent, x_send.at[k]).wait()
        sent = out_rows.at[k, pl.ds(0, group - 1)]
        pltpu.make_async_copy(sent, sent, b_send.at[k]).wait()


def on_device(
    tokens,
    norm_gain,
    expert_ids,
    route_weights,
    gate_weight,
    gate_bias,
    up_weight,
    up_bias,
    down_weight,
    down_bias,
):
    tok_rows, features = tokens.shape
    z_size = Z_RING
    x_size = lax.axis_size("seq") // (z_size * CORES)
    quarter = features // 4
    stages = z_size // 2
    group = x_size * CORES
    rows = group * PAIR

    block = (stages, rows, BLOCK)
    vmem = pl.BlockSpec(memory_space=pltpu.VMEM)
    hbm = pl.BlockSpec(memory_space=pl.ANY)
    dma = pltpu.SemaphoreType.DMA
    mixed = pl.pallas_call(
        functools.partial(kernel, x_size, z_size),
        out_shape=pltpu.VMEM((quarter, tok_rows), BF16),
        in_specs=[hbm] * 10,
        out_specs=vmem,
        scratch_shapes=[
            pltpu.VMEM((features, tok_rows), BF16),
            pltpu.VMEM((features,), F32),
            pltpu.VMEM((4, tok_rows), jnp.int32),
            pltpu.VMEM((4, tok_rows), F32),
            pltpu.VMEM(gate_bias.shape, F32),
            pltpu.VMEM(up_bias.shape, F32),
            pltpu.VMEM(down_bias.shape, F32),
            pltpu.VMEM((8, BLOCK), F32),
            pltpu.VMEM((stages, 2, tok_rows, BLOCK), BF16),
            pltpu.VMEM((stages, 2, 8, tok_rows), F32),
            pltpu.VMEM((stages, group, PAIR, BLOCK), BF16),
            pltpu.VMEM((stages, 4, group, PAIR, BLOCK), BF16),
            pltpu.VMEM((4 * BLOCK, 2 * BLOCK), BF16),
            pltpu.VMEM((BLOCK, 4 * BLOCK), BF16),
            pltpu.VMEM(gate_weight.shape[1:], BF16),
            pltpu.VMEM(up_weight.shape[1:], BF16),
            pltpu.VMEM(down_weight.shape[1:], BF16),
            pltpu.VMEM((stages, 4, rows, BLOCK), BF16),
            pltpu.VMEM(block, BF16),
            pltpu.VMEM(block, BF16),
            pltpu.VMEM(block, BF16),
            pltpu.VMEM(block, BF16),
            pltpu.VMEM((stages, group, PAIR, BLOCK), BF16),
            pltpu.VMEM((stages, group, PAIR, BLOCK), BF16),
            pltpu.VMEM((stages, 2 * tok_rows, 2 * rows), BF16),
            pltpu.VMEM((2, stages, tok_rows, BLOCK), BF16),
            pltpu.VMEM((2, stages, tok_rows, BLOCK), BF16),
            pltpu.VMEM((tok_rows, tok_rows), BF16),
            dma((7,)),
            dma((3,)),
            dma((2, stages, CUTS)),
            dma((2, stages, CUTS)),
            dma((2, stages)),
            dma((2, stages)),
            dma((stages,)),
            dma((stages,)),
            dma((stages,)),
            dma((3, stages, 2)),
            dma((3, stages, 2)),
            dma((3, stages, 2)),
            dma((3, stages, 2)),
            dma((stages,)),
            dma((stages,)),
            dma((stages,)),
            dma((2, stages, CUTS)),
            dma((2, stages, CUTS)),
        ],
        compiler_params=pltpu.CompilerParams(
            collective_id=0, has_side_effects=True, vmem_limit_bytes=56 * 1024 * 1024
        ),
    )(
        tokens.T,
        norm_gain,
        expert_ids.T,
        route_weights.T,
        gate_bias,
        up_bias,
        down_bias,
        gate_weight,
        up_weight,
        down_weight,
    )
    return mixed.T


def solution(mesh):
    placed = (
        P("seq", None),
        P(),
        P("seq", None),
        P("seq", None),
        P("seq", None, "rep"),
        P("seq", "rep"),
        P("seq", None, "rep"),
        P("seq", "rep"),
        P("seq", "rep", None),
        P("seq", "rep"),
    )
    return jax.shard_map(
        on_device, mesh=mesh, in_specs=placed, out_specs=P("seq", "rep"), check_vma=False
    )
```

```python
import functools

import jax
import jax.numpy as jnp
from jax import lax
from jax.experimental import pallas as pl
from jax.experimental.pallas import tpu as pltpu
from jax.sharding import PartitionSpec as P

MESH = pl.DeviceIdType.MESH
BF16, F32 = jnp.bfloat16, jnp.float32

CORES = 2
Z_RING = 16
BLOCK = 384
SLOTS = 8
PAIR = 2 * SLOTS
CUTS = 4


def kernel(
    x_size,
    z_size,
    tokens_hbm,
    gain_hbm,
    ids_hbm,
    route_hbm,
    bg_hbm,
    bu_hbm,
    bd_hbm,
    wg_hbm,
    wu_hbm,
    wd_hbm,
    out_ref,
    tokens_s,
    gain_s,
    ids_s,
    route_s,
    bg_s,
    bu_s,
    bd_s,
    bias_ref,
    tok,
    meta,
    rows_out,
    in_rows,
    w_in,
    w_out,
    wg_s,
    wu_s,
    wd_s,
    part,
    rs_r,
    rs_n,
    rs_t,
    out_rows,
    back,
    mix,
    acc_s,
    acc_r,
    upper,
    i_sem,
    w_sem,
    z_send,
    z_recv,
    m_send,
    m_recv,
    x_send,
    x_recv,
    x_loc,
    y_send,
    y_recv,
    y_near,
    r_send,
    r_recv,
    r_near,
    b_send,
    b_recv,
    b_loc,
    c_send,
    c_recv,
):
    seq, y = lax.axis_index("seq"), lax.axis_index("rep")
    half_z = z_size // 2
    stages = half_z
    group = x_size * CORES
    rows = group * PAIR
    tokens = tok.shape[2]
    piece = tokens // CUTS
    side = group // 2
    quarter = out_ref.shape[0]
    xi = seq // (z_size * CORES)
    zi = (seq // CORES) % z_size
    ci = seq % CORES
    me = xi * CORES + ci

    def at_z(step):
        return (xi * z_size + (zi + z_size + step) % z_size) * CORES + ci

    def at_x(index):
        return ((index // CORES) * z_size + zi) * CORES + index % CORES

    def at_y(step):
        return (y + 4 + step) % 4

    z_up, z_down = at_z(1), at_z(-1)

    small = [
        pltpu.make_async_copy(src, dst, i_sem.at[i])
        for i, (src, dst) in enumerate(
            (
                (tokens_hbm, tokens_s),
                (gain_hbm, gain_s),
                (ids_hbm, ids_s),
                (route_hbm, route_s),
                (bg_hbm, bg_s),
                (bu_hbm, bu_s),
                (bd_hbm, bd_s),
            )
        )
    ]
    for copy in small:
        copy.start()

    barrier = pltpu.get_barrier_semaphore()
    for peer in (z_up, z_down):
        pl.semaphore_signal(barrier, inc=1, device_id=(peer, y), device_id_type=MESH)
    for j in range(1, group):
        pl.semaphore_signal(
            barrier, inc=1, device_id=(at_x((me + j) % group), y), device_id_type=MESH
        )
    for step in (1, -1):
        pl.semaphore_signal(barrier, inc=1, device_id=(seq, at_y(step)), device_id_type=MESH)

    weights = [
        pltpu.make_async_copy(wg_hbm.at[0], wg_s, w_sem.at[0]),
        pltpu.make_async_copy(wu_hbm.at[0], wu_s, w_sem.at[1]),
        pltpu.make_async_copy(wd_hbm.at[0], wd_s, w_sem.at[2]),
    ]
    for copy in weights:
        copy.start()

    def arrived(ref, sem):
        pltpu.make_async_copy(ref, ref, sem).wait()

    def z_copy(way, k, h, src):
        return pltpu.make_async_remote_copy(
            src_ref=src.at[pl.ds(h * piece, piece)],
            dst_ref=tok.at[k, way, pl.ds(h * piece, piece)],
            send_sem=z_send.at[way],
            recv_sem=z_recv.at[way, k, h],
            device_id=(z_up if way else z_down, y),
            device_id_type=MESH,
        )

    def m_copy(way, k, src):
        return pltpu.make_async_remote_copy(
            src_ref=src,
            dst_ref=meta.at[k, way],
            send_sem=m_send.at[way],
            recv_sem=m_recv.at[way, k],
            device_id=(z_up if way else z_down, y),
            device_id_type=MESH,
        )

    for copy in small:
        copy.wait()
    values = tokens_s[...].astype(F32)
    features = values.shape[0]
    scale = lax.rsqrt(jnp.sum(values * values, axis=0, keepdims=True) / features + 1e-05)
    for q in range(4):
        width = min(BLOCK, features - q * BLOCK)

        @pl.when(y == q)
        def _():
            at = slice(q * BLOCK, q * BLOCK + width)
            normed = (tokens_s[at, :].astype(F32) * scale).T * gain_s[at].reshape(1, width)
            if width < BLOCK:
                tok[0, 1] = jnp.zeros((tokens, BLOCK), BF16)
            tok[0, 1, :, 0:width] = normed.astype(BF16)

    meta[0, 1] = jnp.concatenate([ids_s[...].astype(F32), route_s[...]], axis=0)
    pl.semaphore_wait(barrier, 2 + (group - 1) + 2)
    for h in range(CUTS):
        for way in (0, 1):
            z_copy(way, way, h, tok.at[0, 1]).start()
    for way in (0, 1):
        m_copy(way, way, meta.at[0, 1]).start()

    hidden = bg_s.shape[1]
    bias_ref[...] = jnp.zeros_like(bias_ref)
    bias_ref[0:1, 0:hidden] = bg_s[...]
    bias_ref[1:2, 0:hidden] = bu_s[...]
    bias_ref[2:3, 0:quarter] = bd_s[...]
    upper[...] = (
        lax.broadcasted_iota(jnp.int32, (tokens, tokens), 0)
        < lax.broadcasted_iota(jnp.int32, (tokens, tokens), 1)
    ).astype(BF16)

    w_in[...] = jnp.zeros_like(w_in)
    w_out[...] = jnp.zeros_like(w_out)
    for copy in weights:
        copy.wait()
    strip = 144

    @pl.loop(0, features // strip)
    def _(i):
        at = pl.ds(pl.multiple_of(i * strip, 16), strip)
        w_in[at, 0:hidden] = wg_s[at, :]
        w_in[at, BLOCK : BLOCK + hidden] = wu_s[at, :]

    for p in range(4):
        w_out[0:hidden, p * BLOCK : p * BLOCK + quarter] = wd_s[:, p * quarter : (p + 1) * quarter]

    expert = lax.broadcasted_iota(jnp.int32, (group, tokens), 0)
    expert = ((expert // CORES) * z_size + zi) * CORES + expert % CORES
    expert = expert.astype(F32)
    slot = lax.broadcasted_iota(jnp.int32, (group, SLOTS, tokens), 1).astype(F32)

    def x_copy(k, j):
        e = (me + j) % group
        return pltpu.make_async_remote_copy(
            src_ref=rows_out.at[k, e],
            dst_ref=in_rows.at[k, y, me],
            send_sem=x_send.at[0],
            recv_sem=x_recv.at[k],
            device_id=(at_x(e), y),
            device_id_type=MESH,
        )

    def x_local(k):
        return pltpu.make_async_copy(rows_out.at[k, me], in_rows.at[k, y, me], x_loc.at[k])

    def b_copy(k, j):
        e = (me + j) % group
        return pltpu.make_async_remote_copy(
            src_ref=out_rows.at[k, e],
            dst_ref=back.at[k, me],
            send_sem=b_send.at[0],
            recv_sem=b_recv.at[k],
            device_id=(at_x(e), y),
            device_id_type=MESH,
        )

    def b_local(k):
        return pltpu.make_async_copy(out_rows.at[k, me], back.at[k, me], b_loc.at[k])

    def y_copy(k, kind, h):
        s = 1 - 2 * h
        block = at_y(-s) if kind == 2 else y
        at = in_rows.at[k, block, pl.ds(h * side, side)]
        return pltpu.make_async_remote_copy(
            src_ref=at,
            dst_ref=at,
            send_sem=y_send.at[kind],
            recv_sem=y_recv.at[k, h] if kind == 0 else y_near.at[k],
            device_id=(seq, at_y(-s) if kind == 1 else at_y(s)),
            device_id_type=MESH,
        )

    def r_copy(k, kind, h):
        s = 1 - 2 * h
        at = pl.ds(h * (rows // 2), rows // 2)
        src = rs_t.at[k, at] if kind == 2 else part.at[k, at_y(2) if kind == 0 else at_y(-s), at]
        return pltpu.make_async_remote_copy(
            src_ref=src,
            dst_ref=rs_n.at[k, kind - 1, at] if kind else rs_r.at[k, at],
            send_sem=r_send.at[kind],
            recv_sem=r_recv.at[k, h] if kind == 0 else r_near.at[k],
            device_id=(seq, at_y(-s) if kind == 1 else at_y(s)),
            device_id_type=MESH,
        )

    def c_copy(way, k, h, to_slot):
        return pltpu.make_async_remote_copy(
            src_ref=acc_s.at[way, k, pl.ds(h * piece, piece)],
            dst_ref=acc_r.at[way, to_slot, pl.ds(h * piece, piece)],
            send_sem=c_send.at[way],
            recv_sem=c_recv.at[way, to_slot, h],
            device_id=(z_down if way else z_up, y),
            device_id_type=MESH,
        )

    def z_stage(k):
        def step(way, wait, forward):
            def go():
                wait()
                pl.when(k < stages - 1)(forward)

            if way:
                pl.when(k >= 1)(go)
            else:
                go()

        for h in range(CUTS):
            for way in (1, 0):
                step(
                    way,
                    lambda: z_copy(way, k, h, tok.at[k, way]).wait_recv(),
                    lambda: z_copy(way, k + 1, h, tok.at[k, way]).start(),
                )
        for way in (1, 0):
            step(
                way,
                lambda: m_copy(way, k, meta.at[k, way]).wait_recv(),
                lambda: m_copy(way, k + 1, meta.at[k, way]).start(),
            )

    def dispatch(k):
        picks, mixes = [], []
        for j in (0, 1):
            m = meta[k, j]
            hit = jnp.zeros((group, tokens), F32)
            weight = jnp.zeros((group, tokens), F32)
            for c in range(4):
                equal = m[c : c + 1, :] == expert
                hit = jnp.where(equal, 1.0, hit)
                weight = jnp.where(equal, m[4 + c : 5 + c, :], weight)
            rank = jnp.dot(hit.astype(BF16), upper[...], preferred_element_type=F32)
            rank = jnp.where(hit > 0.5, rank, -1.0)
            chosen = rank[:, None, :] == slot
            picks.append(jnp.where(chosen, 1.0, 0.0))
            mixes.append(jnp.where(chosen, weight[:, None, :], 0.0))
        empty = jnp.zeros((group, SLOTS, tokens), F32)

        def both(a, b):
            top = jnp.concatenate([a, empty], axis=2)
            low = jnp.concatenate([empty, b], axis=2)
            return jnp.concatenate([top, low], axis=1).reshape(rows, 2 * tokens)

        pick = both(*picks).astype(BF16)
        got = jnp.dot(pick, tok[k].reshape(2 * tokens, BLOCK), preferred_element_type=F32)
        rows_out[k] = got.astype(BF16).reshape(group, PAIR, BLOCK)
        x_local(k).start()
        for j in range(1, group):
            x_copy(k, j).start()
        blend = both(*mixes).T
        high = blend.astype(BF16)
        mix[k, :, 0:rows] = high
        mix[k, :, rows : 2 * rows] = (blend - high.astype(F32)).astype(BF16)

    def y_start(k):
        x_local(k).wait()
        arrived(in_rows.at[k, y, pl.ds(0, group - 1)], x_recv.at[k])
        for kind in (0, 1):
            for h in (0, 1):
                y_copy(k, kind, h).start()

    def y_relay(k):
        for h in (0, 1):
            y_copy(k, 0, h).wait_recv()
            y_copy(k, 2, h).start()

    def compute(k):
        arrived(in_rows.at[k, pl.ds(0, 2)], y_near.at[k])
        x = jnp.concatenate([in_rows[k, q].reshape(rows, BLOCK) for q in range(4)], axis=1)
        pre = jnp.dot(x, w_in[...], preferred_element_type=F32)
        gate = pre[:, :BLOCK] + bias_ref[0:1, :]
        up = pre[:, BLOCK:] + bias_ref[1:2, :]
        act = (gate * jax.nn.sigmoid(1.702 * gate) * (up + 1.0)).astype(BF16)
        result = jnp.dot(act, w_out[...], preferred_element_type=F32).astype(BF16)
        for p in range(4):
            part[k, p] = result[:, p * BLOCK : (p + 1) * BLOCK]

    def stage(t, first, go):
        pl.when((t >= first) & (t < stages + first))(lambda: go(t - first))

    @pl.loop(0, stages + 5)
    def _(t):
        stage(t, 0, z_stage)
        stage(t, 3, y_relay)
        stage(t, 0, dispatch)
        stage(t, 1, y_start)
        stage(t, 5, compute)

    def r_start(k, kind):
        for h in (0, 1):
            r_copy(k, kind, h).start()

    def r_relay(k):
        for h in (0, 1):
            at = pl.ds(h * (rows // 2), rows // 2)
            r_copy(k, 0, h).wait_recv()
            total = rs_r[k, at].astype(F32) + part[k, at_y(1 - 2 * h), at].astype(F32)
            rs_t[k, at] = total.astype(BF16)
            r_copy(k, 2, h).start()

    def finish(k):
        arrived(rs_n.at[k], r_near.at[k])
        total = part[k, y].astype(F32) + rs_n[k, 0].astype(F32) + rs_n[k, 1].astype(F32)
        total = total + bias_ref[2:3, :]
        out_rows[k] = total.astype(BF16).reshape(group, PAIR, BLOCK)
        b_local(k).start()
        for j in range(1, group):
            b_copy(k, j).start()

    def combine(k):
        b_local(k).wait()
        arrived(back.at[k, pl.ds(0, group - 1)], b_recv.at[k])
        came = back[k].reshape(rows, BLOCK)
        came = jnp.concatenate([came, came], axis=0)
        both = jnp.dot(mix[k], came, preferred_element_type=F32)
        for h in range(CUTS):
            at = pl.ds(h * piece, piece)
            for way in (0, 1):
                first = way * tokens + h * piece
                value = both[first : first + piece]

                @pl.when(k == stages - 1)
                def _():
                    acc_s[way, k, at] = value.astype(BF16)

                @pl.when(k < stages - 1)
                def _():
                    c_copy(way, k, h, k).wait_recv()
                    total = value + acc_r[way, k, at].astype(F32)
                    acc_s[way, k, at] = total.astype(BF16)

                if way == 0:
                    c_copy(0, k, h, (k + stages - 1) % stages).start()
                else:

                    @pl.when(k >= 1)
                    def _():
                        c_copy(1, k, h, k - 1).start()

        @pl.when(k == 0)
        def _():
            for h in range(CUTS):
                c_copy(0, 0, h, stages - 1).wait_recv()
            total = both[tokens:] + acc_r[1, 0].astype(F32) + acc_r[0, stages - 1].astype(F32)
            out_ref[...] = total.T[:quarter].astype(out_ref.dtype)

    def turn(go):
        return lambda n: go(stages - 1 - n)

    @pl.loop(0, stages + 4)
    def _(t):
        stage(t, 0, turn(lambda k: r_start(k, 0)))
        stage(t, 3, turn(finish))
        stage(t, 1, turn(lambda k: r_start(k, 1)))
        stage(t, 1, turn(r_relay))
        stage(t, 4, turn(combine))

    for way in (0, 1):
        sent = pl.ds(0, stages - way)
        arrived(meta.at[sent, way], m_send.at[way])
        arrived(tok.at[sent, way], z_send.at[way])
        arrived(acc_s.at[way, sent], c_send.at[way])
    for kind in range(3):
        arrived(in_rows.at[:, y], y_send.at[kind])
        arrived(rs_r, r_send.at[kind])
    arrived(rows_out.at[:, pl.ds(0, group - 1)], x_send.at[0])
    arrived(out_rows.at[:, pl.ds(0, group - 1)], b_send.at[0])


def on_device(
    tokens,
    norm_gain,
    expert_ids,
    route_weights,
    gate_weight,
    gate_bias,
    up_weight,
    up_bias,
    down_weight,
    down_bias,
):
    tok_rows, features = tokens.shape
    z_size = Z_RING
    x_size = lax.axis_size("seq") // (z_size * CORES)
    quarter = features // 4
    stages = z_size // 2
    group = x_size * CORES
    rows = group * PAIR

    block = (stages, rows, BLOCK)
    vmem = pl.BlockSpec(memory_space=pltpu.VMEM)
    hbm = pl.BlockSpec(memory_space=pl.ANY)
    dma = pltpu.SemaphoreType.DMA
    mixed = pl.pallas_call(
        functools.partial(kernel, x_size, z_size),
        out_shape=pltpu.VMEM((quarter, tok_rows), BF16),
        in_specs=[hbm] * 10,
        out_specs=vmem,
        scratch_shapes=[
            pltpu.VMEM((features, tok_rows), BF16),
            pltpu.VMEM((features,), F32),
            pltpu.VMEM((4, tok_rows), jnp.int32),
            pltpu.VMEM((4, tok_rows), F32),
            pltpu.VMEM(gate_bias.shape, F32),
            pltpu.VMEM(up_bias.shape, F32),
            pltpu.VMEM(down_bias.shape, F32),
            pltpu.VMEM((8, BLOCK), F32),
            pltpu.VMEM((stages, 2, tok_rows, BLOCK), BF16),
            pltpu.VMEM((stages, 2, 8, tok_rows), F32),
            pltpu.VMEM((stages, group, PAIR, BLOCK), BF16),
            pltpu.VMEM((stages, 4, group, PAIR, BLOCK), BF16),
            pltpu.VMEM((4 * BLOCK, 2 * BLOCK), BF16),
            pltpu.VMEM((BLOCK, 4 * BLOCK), BF16),
            pltpu.VMEM(gate_weight.shape[1:], BF16),
            pltpu.VMEM(up_weight.shape[1:], BF16),
            pltpu.VMEM(down_weight.shape[1:], BF16),
            pltpu.VMEM((stages, 4, rows, BLOCK), BF16),
            pltpu.VMEM(block, BF16),
            pltpu.VMEM((stages, 2, rows, BLOCK), BF16),
            pltpu.VMEM(block, BF16),
            pltpu.VMEM((stages, group, PAIR, BLOCK), BF16),
            pltpu.VMEM((stages, group, PAIR, BLOCK), BF16),
            pltpu.VMEM((stages, 2 * tok_rows, 2 * rows), BF16),
            pltpu.VMEM((2, stages, tok_rows, BLOCK), BF16),
            pltpu.VMEM((2, stages, tok_rows, BLOCK), BF16),
            pltpu.VMEM((tok_rows, tok_rows), BF16),
            dma((7,)),
            dma((3,)),
            dma((2,)),
            dma((2, stages, CUTS)),
            dma((2,)),
            dma((2, stages)),
            dma((1,)),
            dma((stages,)),
            dma((stages,)),
            dma((3,)),
            dma((stages, 2)),
            dma((stages,)),
            dma((3,)),
            dma((stages, 2)),
            dma((stages,)),
            dma((1,)),
            dma((stages,)),
            dma((stages,)),
            dma((2,)),
            dma((2, stages, CUTS)),
        ],
        compiler_params=pltpu.CompilerParams(
            collective_id=0, has_side_effects=True, vmem_limit_bytes=56 * 1024 * 1024
        ),
    )(
        tokens.T,
        norm_gain,
        expert_ids.T,
        route_weights.T,
        gate_bias,
        up_bias,
        down_bias,
        gate_weight,
        up_weight,
        down_weight,
    )
    return mixed.T


def solution(mesh):
    placed = (
        P("seq", None),
        P(),
        P("seq", None),
        P("seq", None),
        P("seq", None, "rep"),
        P("seq", "rep"),
        P("seq", None, "rep"),
        P("seq", "rep"),
        P("seq", "rep", None),
        P("seq", "rep"),
    )
    return jax.shard_map(
        on_device, mesh=mesh, in_specs=placed, out_specs=P("seq", "rep"), check_vma=False
    )
```
